32 devices in a mesh: sub: 8 (over z, x), panel: 4 (over y, core).
Axes of the slice: x: 2, y: 2, z: 4, core: 2. Of those that a mesh axis runs over, the one named last changes fastest.
Arguments:
- border_factor: bfloat16 [8, 1024, 4096], P('sub', None, 'panel'), may hold values from -0.119628906 to 0.119628906
- tile_mask: int32 [8, 8, 32], P('sub', None, 'panel'), may hold values 0 or 1
- front_maps: int32 [3, 8, 1024], replicated, may hold values from 0 to 1279, as said below
- sep_inverse: float32 [3, 256, 256], replicated, may hold values from -1 to 5, as said below
- sep_scale: float32 [3, 8, 256], replicated, may hold values from 0.25 to 1.75
Outputs:
- border_schur: float32 [8, 1024, 1024], P('sub', 'panel')
The draws below stay inside these ranges and needn't reach their ends.
Inputs may be any that keep to these rules, and one draw needn't show every extreme that they name: `front_maps`: entry [l, c, i] lies in front block i // 256, that is from (i // 256) * 320 to (i // 256) * 320 + 319, and the 256 entries of one child in one block are distinct. `sep_inverse`: each level's matrix is symmetric.
All inputs are finite; a program needn't handle non-finite values. No bound on the sum of `tile_mask` on one device may be relied on, other than what follows from the above.
Results may differ from the reference program's by a relative error of at most 0.0003.
Values sent between devices are 32-bit elements; how exact they have to be, the bound alone decides.
A program may use at most 64 MiB of HBM per device.

```python
import math
import jax
import jax.numpy as jnp
from jax import lax

BORDER = 1024
SEP = 256
TILE = 128
LEVELS = 3
COLS = 4096
BROWS = 256
FROWS = 320
N_SUB = 8
N_PANEL = 4


def draw_front_maps(key, part):
    scores = jax.random.randint(key, (LEVELS, N_SUB, N_PANEL, FROWS), 0, 1 << 20)
    scores = scores * FROWS + jnp.arange(FROWS, dtype=jnp.int32)
    order = jnp.argsort(scores, axis=-1, stable=True).astype(jnp.int32)
    base = (jnp.arange(N_PANEL, dtype=jnp.int32) * FROWS)[None, None, :, None]
    return (order[..., :BROWS] + base).reshape(LEVELS, N_SUB, BORDER)


def draw_sep_inverse(key, part):
    key_diag = jax.random.fold_in(key, 11)
    key_rough = jax.random.fold_in(key, 23)
    diagonal = jnp.exp(jax.random.uniform(key_diag, (LEVELS, SEP), jnp.float32, 0.0, math.log(4.0)))
    rough = jax.random.uniform(key_rough, (LEVELS, SEP, SEP), jnp.float32, -1.0, 1.0)
    symmetric = 0.5 * (rough + jnp.swapaxes(rough, 1, 2)) / math.sqrt(SEP)
    return symmetric + diagonal[:, :, None] * jnp.eye(SEP, dtype=jnp.float32)[None]


def plant(entries, rng, least, largest):
    index_at = [jax.random.randint(jax.random.fold_in(rng, axis), (), 0, length) for axis, length in enumerate(entries.shape)]
    widest = entries.shape.index(max(entries.shape))
    next_to = index_at[:widest] + [(index_at[widest] + 1) % entries.shape[widest]] + index_at[widest + 1:]
    return entries.at[tuple(index_at)].set(least).at[tuple(next_to)].set(largest)


def raised(drawn, key, source, target, shards_of, factor):
    owner, partner = [(jnp.arange(drawn.shape[axis_at]) // (drawn.shape[axis_at] // shards_of)).reshape([-1 if axis == axis_at else 1 for axis in range(drawn.ndim)]) for axis_at in (source, target)]
    chosen = jax.random.permutation(key, shards_of)[partner]
    strong = (owner == chosen) | (owner == (partner + shards_of // 2) % shards_of)
    return jnp.where(strong, factor * drawn, drawn)


def block_levels(key, dims, shards, low, largest):
    loudness = 1.0
    for position, parts in shards:
        steps = jax.random.uniform(jax.random.fold_in(jax.random.fold_in(key, 6), position), (parts,), jnp.float32, low / len(shards), largest / len(shards))
        loudness = loudness * jnp.repeat(jnp.exp(steps), dims[position] // parts).reshape((-1,) + (1,) * (len(dims) - 1 - position))
    return loudness


def heavy_noise(stream_key, extent, scale, limit, shards, heavy, kind=jnp.bfloat16):
    drawn = scale * jax.random.normal(stream_key, extent, jnp.float32)
    if shards:
        drawn = drawn * block_levels(stream_key, extent, shards, -0.22, 0.18)
    return jnp.clip(raised(drawn, jax.random.fold_in(stream_key, 3), *heavy), -limit, limit).astype(kind)


def setup_inputs(seed: int = 0) -> dict:
    splits = jax.random.split(jax.random.key(seed), 6)
    return {
        "border_factor": heavy_noise(splits[0], (N_SUB, BORDER, COLS), 0.02, 0.119628906, ((0, 8), (2, 4)), (2, 1, 4, 2.0)),
        "tile_mask": plant((jax.random.randint(splits[1], (N_SUB, BORDER // TILE, COLS // TILE), 0, 2) < 1).astype(jnp.int32), jax.random.fold_in(splits[1], 1), 0, 1),
        "front_maps": draw_front_maps(jax.random.fold_in(splits[5], 71), 0),
        "sep_inverse": draw_sep_inverse(jax.random.fold_in(splits[5], 71), 0),
        "sep_scale": jnp.clip(1.0 + 0.15 * jax.random.normal(splits[4], (LEVELS, N_SUB, SEP), jnp.float32), 0.25, 1.75),
    }


def spread_child(block, child_map, positions):
    onehot = (child_map[:, None] == positions[None, :]).astype(jnp.float32)
    lifted = jnp.dot(onehot.T, block, precision=lax.Precision.HIGHEST, preferred_element_type=jnp.float32)
    return jnp.dot(lifted, onehot, precision=lax.Precision.HIGHEST, preferred_element_type=jnp.float32)


def reference(border_factor, tile_mask, front_maps, sep_inverse, sep_scale):
    tiles = BORDER // TILE

    def leaf(item):
        factor, mask = item
        col_tiles = mask.shape[1]
        masked = (factor.reshape(tiles, TILE, col_tiles, TILE) * mask[:, None, :, None].astype(jnp.bfloat16)).reshape(BORDER, col_tiles * TILE)
        return lax.dot_general(masked, masked, (((1,), (1,)), ((), ())), preferred_element_type=jnp.float32)

    schur = lax.map(leaf, (border_factor, tile_mask))
    srows = SEP // N_PANEL
    brows = BORDER // N_PANEL
    fronts = (SEP + BORDER) // N_PANEL
    sep_index = jnp.arange(SEP, dtype=jnp.int32)
    sep_target = (sep_index // srows) * fronts + sep_index % srows
    border_index = jnp.arange(BORDER, dtype=jnp.int32)
    border_target = (border_index // brows) * fronts + srows + border_index % brows
    positions = jnp.arange(SEP + BORDER, dtype=jnp.int32)
    for level in range(LEVELS):
        groups = schur.shape[0] // 2
        pairs = schur.reshape(groups, 2, BORDER, BORDER)
        pair_maps = front_maps[level, :2 * groups].reshape(groups, 2, BORDER)
        gains = sep_scale[level, :groups]
        inverse = sep_inverse[level]

        def merge(item, inverse=inverse):
            pair, maps_here, gain = item
            front = spread_child(pair[0], maps_here[0], positions) + spread_child(pair[1], maps_here[1], positions)
            border_rows = front[border_target]
            front_sep = border_rows[:, sep_target]
            front_border = border_rows[:, border_target]
            pivot_inverse = gain[:, None] * inverse * gain[None, :]
            coupled = jnp.dot(front_sep, pivot_inverse, precision=lax.Precision.HIGHEST, preferred_element_type=jnp.float32)
            return front_border - jnp.dot(coupled, front_sep.T, precision=lax.Precision.HIGHEST, preferred_element_type=jnp.float32)

        schur = lax.map(merge, (pairs, pair_maps, gains))
    return jnp.repeat(schur, 2 ** LEVELS, axis=0)
```

```python
import functools

import jax
import jax.numpy as jnp
from jax import lax
from jax.experimental import pallas as pl
from jax.experimental.pallas import tpu as pltpu
from jax.sharding import PartitionSpec as P

BORDER = 1024
SEP = 256
TILE = 128
LEVELS = 3
CORES = 2
QUARTERS = 4
F32 = jnp.float32
BF16 = jnp.bfloat16


def nn(a, b):
    return lax.dot_general(a, b, (((1,), (0,)), ((), ())), preferred_element_type=F32)


def nt(a, b):
    return lax.dot_general(a, b, (((1,), (1,)), ((), ())), preferred_element_type=F32)


def split(x):
    high = x.astype(BF16)
    return high, (x - high.astype(F32)).astype(BF16)


def product(a, b):
    a_high, a_low = split(a)
    b_high, b_low = split(b)
    return nn(a_high, b_high) + nn(a_high, b_low) + nn(a_low, b_high)


def kernel(
    panels,
    mask_ref,
    factor_ref,
    maps_ref,
    inverse_ref,
    scale_ref,
    out_ref,
    masked,
    a_send,
    a_recv,
    own,
    b_send,
    b_recv,
    c_send,
    c_recv,
    w0,
    w1,
    w2,
    v0,
    v1,
    v2,
    bb0,
    d_send,
    d_recv,
    e_send,
    e_recv,
    fin,
    send_sem,
    recv_sem,
):
    chips = panels // CORES
    brows = BORDER // panels
    srows = SEP // panels
    fronts = brows + srows
    quarter = BORDER // QUARTERS
    qsep = SEP // QUARTERS
    p = lax.axis_index("panel")
    s = lax.axis_index("sub")
    y, core = p // CORES, p % CORES
    bit0, bit1, bit2 = s % 2, s // 2 % 2, s // 4 % 2
    base = s - s % 8
    sub1 = base + bit2 * 4 + bit1 * 2 + (1 - bit0)
    sub2 = base + bit2 * 4 + (1 - bit1) * 2 + bit0
    sub3 = base + bit2 * 4 + (1 - bit1) * 2 + (1 - bit0)
    sub4 = base + (1 - bit2) * 4 + bit1 * 2 + bit0
    partner = y * CORES + 1 - core
    others = [(y + d) % chips for d in range(1, chips)]

    barrier = pltpu.get_barrier_semaphore()
    greeted = [{"panel": partner}] + [
        {"panel": other * CORES + core} for other in others
    ] + [{"sub": sub} for sub in (sub1, sub2, sub3, sub4)]
    for device in greeted:
        pl.semaphore_signal(barrier, inc=1, device_id=device, device_id_type=pl.DeviceIdType.MESH)

    started = []

    def send(src, dst, device):
        at = len(started)
        copy = pltpu.make_async_remote_copy(
            src_ref=src,
            dst_ref=dst,
            send_sem=send_sem.at[at],
            recv_sem=recv_sem.at[at],
            device_id=device,
            device_id_type=pl.DeviceIdType.MESH,
        )
        copy.start()
        started.append(copy)
        return copy

    for i in range(mask_ref.shape[1]):
        for j in range(mask_ref.shape[2]):
            keep = jnp.full((TILE, TILE), mask_ref[0, i, j].astype(F32), F32).astype(BF16)
            rows, cols = pl.ds(i * TILE, TILE), pl.ds(j * TILE, TILE)
            masked[rows, cols] = factor_ref[0, rows, cols] * keep

    def rows_of(chip, core_there):
        start = pl.multiple_of((chip * CORES + core_there) * brows, brows)
        return masked[pl.ds(start, brows), :]

    first = 2 * (1 - bit0)
    second = 2 * bit0
    order = (first, first + 1, second, second + 1)
    a_copies, b_copies = [], []

    def forward(k):
        a_copies[k].wait_recv()
        copies = []
        for d, other in enumerate(others):
            b_send[k, d] = own[k, other] + a_recv[k, other]
            copies.append(send(b_send.at[k, d], b_recv.at[k, d], {"panel": other * CORES + core}))
        b_copies.append(copies)

    for k, q in enumerate(order):
        columns = masked[pl.ds(pl.multiple_of(q * quarter, quarter), quarter), :]
        for chip in range(chips):
            a_send[k, chip] = nt(rows_of(chip, 1 - core), columns)
        if k == 0:
            pl.semaphore_wait(barrier, len(greeted))
        a_copies.append(send(a_send.at[k], a_recv.at[k], {"panel": partner}))
        for chip in range(chips):
            own[k, chip] = nt(rows_of(chip, core), columns)
        if k:
            forward(k - 1)
    forward(len(order) - 1)

    def map_of(level, child, start, size):
        rows = maps_ref[level, :, pl.ds(start, size)]
        at = lax.broadcasted_iota(jnp.int32, rows.shape, 0)
        return jnp.sum(jnp.where(at == child, rows, 0), axis=0, keepdims=True)

    def row_spread(level, child):
        window = max(brows, 128)
        start = pl.multiple_of(p * brows // window * window, 128)
        row = map_of(level, child, start, window)
        picked = row[:, :brows]
        for t in range(1, window // brows):
            here = (p % (window // brows)) == t
            picked = jnp.where(here, row[:, t * brows : (t + 1) * brows], picked)
        r = picked - p * fronts
        target = jnp.where(r >= srows, r - srows, brows + r)
        at = lax.broadcasted_iota(jnp.int32, (fronts, brows), 0)
        return jnp.where(at == target, 1.0, 0.0).astype(BF16)

    def column_spread(level, child, q):
        start = pl.multiple_of(q * quarter, quarter)
        row = map_of(level, child, start, quarter)
        block = lax.broadcasted_iota(jnp.int32, (1, quarter), 1) // brows
        r = row - (q * (quarter // brows) + block) * fronts
        target = jnp.where(r >= srows, block * brows + r - srows, quarter + block * srows + r)
        at = lax.broadcasted_iota(jnp.int32, (quarter + qsep, quarter), 0)
        return jnp.where(at == target, 1.0, 0.0).astype(BF16)

    def place(block, rows, columns):
        high, low = split(block)
        lifted = nn(rows, high) + nn(rows, low)
        high, low = split(lifted)
        border, sep = columns[:quarter], columns[quarter:]
        spread = nt(high, border) + nt(low, border)
        coupling = nt(sep, high[:brows]) + nt(sep, low[:brows])
        return spread, coupling

    def share_rows(w):
        mine = w.at[p]
        near = send(mine, mine, {"panel": partner})
        far = [
            (other * CORES + core, send(mine, mine, {"panel": other * CORES + core}))
            for other in others
        ]
        return near, far

    def relay_rows(w, near, far):
        relays = []
        for d, (_, copy) in enumerate(far, 1):
            copy.wait_recv()
            slot = w.at[(y + chips - d) % chips * CORES + core]
            relays.append(send(slot, slot, {"panel": partner}))
        near.wait_recv()
        for relay in relays:
            relay.wait_recv()

    def coupled_rows(level, v):
        front = s // 2 ** (level + 1)
        gains = scale_ref[level, pl.ds(front, 1), :]
        rows = jnp.transpose(v[...].reshape(SEP, brows))
        return product(rows * gains, inverse_ref[level] * gains)

    child = s
    sibling = sub1
    rows_own, rows_far = row_spread(0, child), row_spread(0, sibling)

    def total(k):
        for copy in b_copies[k]:
            copy.wait_recv()
        value = own[k, y] + a_recv[k, y]
        for d in range(chips - 1):
            value = value + b_recv[k, d]
        return value

    c_copies = []
    for k in range(2):
        c_send[k] = total(k)
        c_copies.append(send(c_send.at[k], c_recv.at[k], {"sub": sub1}))
    for j in range(2):
        q = second + j
        spread_own, coupling_own = place(total(2 + j), rows_own, column_spread(0, child, q))
        c_copies[j].wait_recv()
        spread_far, coupling_far = place(c_recv[j], rows_far, column_spread(0, sibling, q))
        spread = spread_own + spread_far
        bb0[j] = spread[:brows]
        w0[p, j] = spread[brows:]
        v0[q] = coupling_own + coupling_far
    mine = v0.at[pl.ds(second, 2)]
    v_copy = send(mine, mine, {"sub": sub1})
    near, far = share_rows(w0)
    q = 2 * bit0 + bit1
    group = s // 8 * 8
    child1 = s // 2
    sibling1 = s // 4 * 2 + (1 - bit1)
    child2 = s // 4
    sibling2 = s // 8 * 2 + (1 - bit2)
    v_copy.wait_recv()
    coupled = coupled_rows(0, v0)
    relay_rows(w0, near, far)

    def updated(j):
        return bb0[j] - product(coupled, w0[:, j].reshape(SEP, quarter))

    d_send[...] = updated(1 - bit1)
    copy = send(d_send, d_recv, {"sub": sub2})
    schur = updated(bit1)
    for level, child, sibling, received, w, v in (
        (1, child1, sibling1, d_recv, w1, v1),
        (2, child2, sibling2, e_recv, w2, v2),
    ):
        spread_own, coupling_own = place(
            schur, row_spread(level, child), column_spread(level, child, q)
        )
        rows_far, columns_far = row_spread(level, sibling), column_spread(level, sibling, q)
        copy.wait_recv()
        spread_far, coupling_far = place(received[...], rows_far, columns_far)
        spread = spread_own + spread_far
        w[p] = spread[brows:]
        v[q] = coupling_own + coupling_far
        mine = v.at[q]
        v_copies = [send(mine, mine, {"sub": sub}) for sub in (sub1, sub2, sub3)]
        near, far = share_rows(w)
        for v_copy in v_copies:
            v_copy.wait_recv()
        coupled = coupled_rows(level, v)
        relay_rows(w, near, far)
        schur = spread[:brows] - product(coupled, w[...].reshape(SEP, quarter))
        if level == 1:
            e_send[...] = schur
            copy = send(e_send, e_recv, {"sub": sub4})
    fin[q] = schur
    mine = fin.at[q]
    near = send(mine, mine, {"sub": sub1})
    far = send(mine, mine, {"sub": sub2})
    half = brows // 2
    near.wait_recv()
    slot = fin.at[2 * (1 - bit0) + bit1, pl.ds(0, half)]
    upper = send(slot, slot, {"sub": sub2})
    far.wait_recv()
    slot = fin.at[2 * bit0 + 1 - bit1, pl.ds(half, half)]
    lower = send(slot, slot, {"sub": sub1})
    upper.wait_recv()
    lower.wait_recv()
    for t in range(QUARTERS):
        out_ref[0, :, pl.ds(t * quarter, quarter)] = fin[t]
    for copy in started:
        copy.wait_send()


def body(border_factor, tile_mask, front_maps, sep_inverse, sep_scale):
    panels = lax.axis_size("panel")
    chips = panels // CORES
    brows = BORDER // panels
    srows = SEP // panels
    quarter = BORDER // QUARTERS
    qsep = SEP // QUARTERS
    copies = 4 + 4 * (chips - 1) + 2 + 3 * (1 + 2 * (chips - 1)) + 1 + 6 + 2 + 4
    vmem = pl.BlockSpec(memory_space=pltpu.VMEM)
    block = pltpu.VMEM((brows, quarter), F32)
    return pl.pallas_call(
        functools.partial(kernel, panels),
        out_shape=jax.ShapeDtypeStruct((1, brows, BORDER), F32),
        in_specs=[pl.BlockSpec(memory_space=pltpu.SMEM), vmem, vmem, vmem, vmem],
        out_specs=vmem,
        scratch_shapes=[
            pltpu.VMEM((BORDER, border_factor.shape[2]), BF16),
            pltpu.VMEM((4, chips, brows, quarter), F32),
            pltpu.VMEM((4, chips, brows, quarter), F32),
            pltpu.VMEM((4, chips, brows, quarter), F32),
            pltpu.VMEM((4, chips - 1, brows, quarter), F32),
            pltpu.VMEM((4, chips - 1, brows, quarter), F32),
            pltpu.VMEM((2, brows, quarter), F32),
            pltpu.VMEM((2, brows, quarter), F32),
            pltpu.VMEM((panels, 2, srows, quarter), F32),
            pltpu.VMEM((panels, srows, quarter), F32),
            pltpu.VMEM((panels, srows, quarter), F32),
            pltpu.VMEM((QUARTERS, qsep, brows), F32),
            pltpu.VMEM((QUARTERS, qsep, brows), F32),
            pltpu.VMEM((QUARTERS, qsep, brows), F32),
            pltpu.VMEM((2, brows, quarter), F32),
            block,
            block,
            block,
            block,
            pltpu.VMEM((QUARTERS, brows, quarter), F32),
            pltpu.SemaphoreType.DMA((copies,)),
            pltpu.SemaphoreType.DMA((copies,)),
        ],
        compiler_params=pltpu.CompilerParams(
            collective_id=0, has_side_effects=True, vmem_limit_bytes=50 * 2**20
        ),
    )(tile_mask, border_factor, front_maps, sep_inverse, sep_scale)


def solution(mesh):
    return jax.shard_map(
        body,
        mesh=mesh,
        in_specs=(P("sub", None, "panel"), P("sub", None, "panel"), P(), P(), P()),
        out_specs=P("sub", "panel", None),
        check_vma=False,
    )
```

```python
import functools

import jax
import jax.numpy as jnp
from jax import lax
from jax.experimental import pallas as pl
from jax.experimental.pallas import tpu as pltpu
from jax.sharding import PartitionSpec as P

BORDER = 1024
SEP = 256
TILE = 128
LEVELS = 3
CORES = 2
QUARTERS = 4
F32 = jnp.float32
BF16 = jnp.bfloat16


def nn(a, b):
    return lax.dot_general(a, b, (((1,), (0,)), ((), ())), preferred_element_type=F32)


def nt(a, b):
    return lax.dot_general(a, b, (((1,), (1,)), ((), ())), preferred_element_type=F32)


def split(x):
    high = x.astype(BF16)
    return high, (x - high.astype(F32)).astype(BF16)


def product(a, b):
    a_high, a_low = split(a)
    b_high, b_low = split(b)
    return nn(a_high, b_high) + nn(a_high, b_low) + nn(a_low, b_high)


def kernel(
    panels,
    mask_hbm,
    factor_hbm,
    maps_hbm,
    inverse_hbm,
    scale_hbm,
    out_ref,
    mask_ref,
    factor_ref,
    maps_ref,
    inverse_ref,
    scale_ref,
    load_sem,
    masked,
    a_send,
    a_recv,
    own,
    b_send,
    b_recv,
    c_send,
    c_recv,
    w0,
    w1,
    w2,
    v0,
    v1,
    v2,
    bb0,
    d_send,
    d_recv,
    e_send,
    e_recv,
    fin,
    send_sem,
    recv_sem,
):
    chips = panels // CORES
    brows = BORDER // panels
    srows = SEP // panels
    fronts = brows + srows
    quarter = BORDER // QUARTERS
    qsep = SEP // QUARTERS
    p = lax.axis_index("panel")
    s = lax.axis_index("sub")
    y, core = p // CORES, p % CORES
    bit0, bit1, bit2 = s % 2, s // 2 % 2, s // 4 % 2
    base = s - s % 8
    sub1 = base + bit2 * 4 + bit1 * 2 + (1 - bit0)
    sub2 = base + bit2 * 4 + (1 - bit1) * 2 + bit0
    sub3 = base + bit2 * 4 + (1 - bit1) * 2 + (1 - bit0)
    sub4 = base + (1 - bit2) * 4 + bit1 * 2 + bit0
    partner = y * CORES + 1 - core
    others = [(y + d) % chips for d in range(1, chips)]

    loads = [pltpu.make_async_copy(mask_hbm.at[0], mask_ref, load_sem.at[0])]
    for i in range(QUARTERS):
        rows = pl.ds(i * quarter, quarter)
        loads.append(
            pltpu.make_async_copy(factor_hbm.at[0, rows], factor_ref.at[rows], load_sem.at[1 + i])
        )
    for i, (src, dst) in enumerate(
        ((maps_hbm, maps_ref), (inverse_hbm, inverse_ref), (scale_hbm, scale_ref))
    ):
        loads.append(pltpu.make_async_copy(src, dst, load_sem.at[1 + QUARTERS + i]))
    for load in loads:
        load.start()

    barrier = pltpu.get_barrier_semaphore()
    greeted = [{"panel": partner}] + [
        {"panel": other * CORES + core} for other in others
    ] + [{"sub": sub} for sub in (sub1, sub2, sub3, sub4)]
    for device in greeted:
        pl.semaphore_signal(barrier, inc=1, device_id=device, device_id_type=pl.DeviceIdType.MESH)

    started = []

    def send(src, dst, device):
        at = len(started)
        copy = pltpu.make_async_remote_copy(
            src_ref=src,
            dst_ref=dst,
            send_sem=send_sem.at[at],
            recv_sem=recv_sem.at[at],
            device_id=device,
            device_id_type=pl.DeviceIdType.MESH,
        )
        copy.start()
        started.append(copy)
        return copy

    loads[0].wait()
    for i in range(mask_ref.shape[0]):
        if i % (quarter // TILE) == 0:
            loads[1 + i // (quarter // TILE)].wait()
        for j in range(mask_ref.shape[1]):
            keep = jnp.full((TILE, TILE), mask_ref[i, j].astype(F32), F32).astype(BF16)
            rows, cols = pl.ds(i * TILE, TILE), pl.ds(j * TILE, TILE)
            masked[rows, cols] = factor_ref[rows, cols] * keep

    def rows_of(chip, core_there):
        start = pl.multiple_of((chip * CORES + core_there) * brows, brows)
        return masked[pl.ds(start, brows), :]

    first = 2 * (1 - bit0)
    second = 2 * bit0
    order = (first, first + 1, second, second + 1)
    a_copies, b_copies, near_copies = [], [], []
    near_chip = y

    def columns_of(q):
        return masked[pl.ds(pl.multiple_of(q * quarter, quarter), quarter), :]

    def forward(k):
        copies = []
        for d, other in enumerate(others):
            a_copies[k][d].wait_recv()
            b_send[k, d] = own[k, other] + a_recv[k, other]
            copies.append(send(b_send.at[k, d], b_recv.at[k, d], {"panel": other * CORES + core}))
        b_copies.append(copies)

    for k, q in enumerate(order):
        copies = []
        for other in others:
            a_send[k, other] = nt(rows_of(other, 1 - core), columns_of(q))
            if not started:
                pl.semaphore_wait(barrier, len(greeted))
            copies.append(send(a_send.at[k, other], a_recv.at[k, other], {"panel": partner}))
        a_copies.append(copies)
        for other in others:
            own[k, other] = nt(rows_of(other, core), columns_of(q))
        if k:
            forward(k - 1)
    forward(len(order) - 1)
    for k, q in enumerate(order):
        a_send[k, near_chip] = nt(rows_of(near_chip, 1 - core), columns_of(q))
        near_copies.append(
            send(a_send.at[k, near_chip], a_recv.at[k, near_chip], {"panel": partner})
        )
        own[k, near_chip] = nt(rows_of(near_chip, core), columns_of(q))
    for load in loads[1 + QUARTERS :]:
        load.wait()

    def map_of(level, child, start, size):
        rows = maps_ref[level, :, pl.ds(start, size)]
        at = lax.broadcasted_iota(jnp.int32, rows.shape, 0)
        return jnp.sum(jnp.where(at == child, rows, 0), axis=0, keepdims=True)

    def row_spread(level, child):
        window = max(brows, 128)
        start = pl.multiple_of(p * brows // window * window, 128)
        row = map_of(level, child, start, window)
        picked = row[:, :brows]
        for t in range(1, window // brows):
            here = (p % (window // brows)) == t
            picked = jnp.where(here, row[:, t * brows : (t + 1) * brows], picked)
        r = picked - p * fronts
        target = jnp.where(r >= srows, r - srows, brows + r)
        at = lax.broadcasted_iota(jnp.int32, (fronts, brows), 0)
        return jnp.where(at == target, 1.0, 0.0).astype(BF16)

    def column_spread(level, child, q):
        start = pl.multiple_of(q * quarter, quarter)
        row = map_of(level, child, start, quarter)
        block = lax.broadcasted_iota(jnp.int32, (1, quarter), 1) // brows
        r = row - (q * (quarter // brows) + block) * fronts
        target = jnp.where(r >= srows, block * brows + r - srows, quarter + block * srows + r)
        at = lax.broadcasted_iota(jnp.int32, (quarter + qsep, quarter), 0)
        return jnp.where(at == target, 1.0, 0.0).astype(BF16)

    def place(block, rows, columns):
        high, low = split(block)
        lifted = nn(rows, high) + nn(rows, low)
        high, low = split(lifted)
        border, sep = columns[:quarter], columns[quarter:]
        spread = nt(high, border) + nt(low, border)
        coupling = nt(sep, high[:brows]) + nt(sep, low[:brows])
        return spread, coupling

    def share_rows(w):
        mine = w.at[p]
        near = send(mine, mine, {"panel": partner})
        far = [
            (other * CORES + core, send(mine, mine, {"panel": other * CORES + core}))
            for other in others
        ]
        return near, far

    def relay_rows(w, near, far):
        relays = []
        for d, (_, copy) in enumerate(far, 1):
            copy.wait_recv()
            slot = w.at[(y + chips - d) % chips * CORES + core]
            relays.append(send(slot, slot, {"panel": partner}))
        near.wait_recv()
        for relay in relays:
            relay.wait_recv()

    def coupled_rows(level, v):
        front = s // 2 ** (level + 1)
        gains = scale_ref[level, pl.ds(front, 1), :]
        rows = jnp.transpose(v[...].reshape(SEP, brows))
        return product(rows * gains, inverse_ref[level] * gains)

    child = s
    sibling = sub1
    rows_own, rows_far = row_spread(0, child), row_spread(0, sibling)

    def total(k):
        near_copies[k].wait_recv()
        for copy in b_copies[k]:
            copy.wait_recv()
        value = own[k, y] + a_recv[k, y]
        for d in range(chips - 1):
            value = value + b_recv[k, d]
        return value

    c_copies = []
    for k in range(2):
        c_send[k] = total(k)
        c_copies.append(send(c_send.at[k], c_recv.at[k], {"sub": sub1}))
    for j in range(2):
        q = second + j
        spread_own, coupling_own = place(total(2 + j), rows_own, column_spread(0, child, q))
        c_copies[j].wait_recv()
        spread_far, coupling_far = place(c_recv[j], rows_far, column_spread(0, sibling, q))
        spread = spread_own + spread_far
        bb0[j] = spread[:brows]
        w0[p, j] = spread[brows:]
        v0[q] = coupling_own + coupling_far
    mine = v0.at[pl.ds(second, 2)]
    v_copy = send(mine, mine, {"sub": sub1})
    near, far = share_rows(w0)
    q = 2 * bit0 + bit1
    group = s // 8 * 8
    child1 = s // 2
    sibling1 = s // 4 * 2 + (1 - bit1)
    child2 = s // 4
    sibling2 = s // 8 * 2 + (1 - bit2)
    v_copy.wait_recv()
    coupled = coupled_rows(0, v0)
    relay_rows(w0, near, far)

    def updated(j):
        return bb0[j] - product(coupled, w0[:, j].reshape(SEP, quarter))

    d_send[...] = updated(1 - bit1)
    copy = send(d_send, d_recv, {"sub": sub2})
    schur = updated(bit1)
    for level, child, sibling, received, w, v in (
        (1, child1, sibling1, d_recv, w1, v1),
        (2, child2, sibling2, e_recv, w2, v2),
    ):
        spread_own, coupling_own = place(
            schur, row_spread(level, child), column_spread(level, child, q)
        )
        rows_far, columns_far = row_spread(level, sibling), column_spread(level, sibling, q)
        copy.wait_recv()
        spread_far, coupling_far = place(received[...], rows_far, columns_far)
        spread = spread_own + spread_far
        w[p] = spread[brows:]
        v[q] = coupling_own + coupling_far
        mine = v.at[q]
        v_copies = [send(mine, mine, {"sub": sub}) for sub in (sub1, sub2, sub3)]
        near, far = share_rows(w)
        for v_copy in v_copies:
            v_copy.wait_recv()
        coupled = coupled_rows(level, v)
        relay_rows(w, near, far)
        schur = spread[:brows] - product(coupled, w[...].reshape(SEP, quarter))
        if level == 1:
            e_send[...] = schur
            copy = send(e_send, e_recv, {"sub": sub4})
    fin[q] = schur
    mine = fin.at[q]
    near = send(mine, mine, {"sub": sub1})
    far = send(mine, mine, {"sub": sub2})
    half = brows // 2
    near.wait_recv()
    slot = fin.at[2 * (1 - bit0) + bit1, pl.ds(0, half)]
    upper = send(slot, slot, {"sub": sub2})
    far.wait_recv()
    slot = fin.at[2 * bit0 + 1 - bit1, pl.ds(half, half)]
    lower = send(slot, slot, {"sub": sub1})
    upper.wait_recv()
    lower.wait_recv()
    for t in range(QUARTERS):
        out_ref[0, :, pl.ds(t * quarter, quarter)] = fin[t]
    for copy in started:
        copy.wait_send()


def body(border_factor, tile_mask, front_maps, sep_inverse, sep_scale):
    panels = lax.axis_size("panel")
    chips = panels // CORES
    brows = BORDER // panels
    srows = SEP // panels
    quarter = BORDER // QUARTERS
    qsep = SEP // QUARTERS
    copies = 4 + 8 * (chips - 1) + 2 + 3 * (1 + 2 * (chips - 1)) + 1 + 6 + 2 + 4
    vmem = pl.BlockSpec(memory_space=pltpu.VMEM)
    hbm = pl.BlockSpec(memory_space=pltpu.HBM)
    block = pltpu.VMEM((brows, quarter), F32)
    return pl.pallas_call(
        functools.partial(kernel, panels),
        out_shape=jax.ShapeDtypeStruct((1, brows, BORDER), F32),
        in_specs=[hbm] * 5,
        out_specs=vmem,
        scratch_shapes=[
            pltpu.SMEM(tile_mask.shape[1:], jnp.int32),
            pltpu.VMEM(border_factor.shape[1:], BF16),
            pltpu.VMEM(front_maps.shape, jnp.int32),
            pltpu.VMEM(sep_inverse.shape, F32),
            pltpu.VMEM(sep_scale.shape, F32),
            pltpu.SemaphoreType.DMA((1 + QUARTERS + 3,)),
            pltpu.VMEM((BORDER, border_factor.shape[2]), BF16),
            pltpu.VMEM((4, chips, brows, quarter), F32),
            pltpu.VMEM((4, chips, brows, quarter), F32),
            pltpu.VMEM((4, chips, brows, quarter), F32),
            pltpu.VMEM((4, chips - 1, brows, quarter), F32),
            pltpu.VMEM((4, chips - 1, brows, quarter), F32),
            pltpu.VMEM((2, brows, quarter), F32),
            pltpu.VMEM((2, brows, quarter), F32),
            pltpu.VMEM((panels, 2, srows, quarter), F32),
            pltpu.VMEM((panels, srows, quarter), F32),
            pltpu.VMEM((panels, srows, quarter), F32),
            pltpu.VMEM((QUARTERS, qsep, brows), F32),
            pltpu.VMEM((QUARTERS, qsep, brows), F32),
            pltpu.VMEM((QUARTERS, qsep, brows), F32),
            pltpu.VMEM((2, brows, quarter), F32),
            block,
            block,
            block,
            block,
            pltpu.VMEM((QUARTERS, brows, quarter), F32),
            pltpu.SemaphoreType.DMA((copies,)),
            pltpu.SemaphoreType.DMA((copies,)),
        ],
        compiler_params=pltpu.CompilerParams(
            collective_id=0, has_side_effects=True, vmem_limit_bytes=50 * 2**20
        ),
    )(tile_mask, border_factor, front_maps, sep_inverse, sep_scale)


def solution(mesh):
    return jax.shard_map(
        body,
        mesh=mesh,
        in_specs=(P("sub", None, "panel"), P("sub", None, "panel"), P(), P(), P()),
        out_specs=P("sub", "panel", None),
        check_vma=False,
    )
```

```python
import functools

import jax
import jax.numpy as jnp
from jax import lax
from jax.experimental import pallas as pl
from jax.experimental.pallas import tpu as pltpu
from jax.sharding import PartitionSpec as P

BORDER = 1024
SEP = 256
TILE = 128
LEVELS = 3
CORES = 2
QUARTERS = 4
F32 = jnp.float32
BF16 = jnp.bfloat16


def nn(a, b):
    return lax.dot_general(a, b, (((1,), (0,)), ((), ())), preferred_element_type=F32)


def nt(a, b):
    return lax.dot_general(a, b, (((1,), (1,)), ((), ())), preferred_element_type=F32)


def split(x):
    high = x.astype(BF16)
    return high, (x - high.astype(F32)).astype(BF16)


def product(a, b):
    a_high, a_low = split(a)
    b_high, b_low = split(b)
    return nn(a_high, b_high) + nn(a_high, b_low) + nn(a_low, b_high)


def kernel(
    panels,
    mask_hbm,
    factor_hbm,
    maps_hbm,
    inverse_hbm,
    scale_hbm,
    out_ref,
    mask_ref,
    factor_ref,
    maps_ref,
    inverse_ref,
    scale_ref,
    load_sem,
    store_sem,
    masked,
    a_send,
    a_recv,
    own,
    b_send,
    b_recv,
    c_send,
    c_recv,
    w0,
    w1,
    w2,
    v0,
    v1,
    v2,
    bb0,
    d_send,
    d_recv,
    e_send,
    e_recv,
    fin,
    send_sem,
    recv_sem,
):
    chips = panels // CORES
    brows = BORDER // panels
    srows = SEP // panels
    fronts = brows + srows
    quarter = BORDER // QUARTERS
    qsep = SEP // QUARTERS
    p = lax.axis_index("panel")
    s = lax.axis_index("sub")
    y, core = p // CORES, p % CORES
    bit0, bit1, bit2 = s % 2, s // 2 % 2, s // 4 % 2
    base = s - s % 8
    sub1 = base + bit2 * 4 + bit1 * 2 + (1 - bit0)
    sub2 = base + bit2 * 4 + (1 - bit1) * 2 + bit0
    sub3 = base + bit2 * 4 + (1 - bit1) * 2 + (1 - bit0)
    sub4 = base + (1 - bit2) * 4 + bit1 * 2 + bit0
    partner = y * CORES + 1 - core
    others = [(y + d) % chips for d in range(1, chips)]

    loads = [pltpu.make_async_copy(mask_hbm.at[0], mask_ref, load_sem.at[0])]
    for i in range(QUARTERS):
        rows = pl.ds(i * quarter, quarter)
        loads.append(
            pltpu.make_async_copy(factor_hbm.at[0, rows], factor_ref.at[rows], load_sem.at[1 + i])
        )
    for i, (src, dst) in enumerate(
        ((maps_hbm, maps_ref), (inverse_hbm, inverse_ref), (scale_hbm, scale_ref))
    ):
        loads.append(pltpu.make_async_copy(src, dst, load_sem.at[1 + QUARTERS + i]))
    for load in loads:
        load.start()

    barrier = pltpu.get_barrier_semaphore()
    greeted = [{"panel": partner}] + [
        {"panel": other * CORES + core} for other in others
    ] + [{"sub": sub} for sub in (sub1, sub2, sub3, sub4)]
    for device in greeted:
        pl.semaphore_signal(barrier, inc=1, device_id=device, device_id_type=pl.DeviceIdType.MESH)

    started = []

    def send(src, dst, device):
        at = len(started)
        copy = pltpu.make_async_remote_copy(
            src_ref=src,
            dst_ref=dst,
            send_sem=send_sem.at[at],
            recv_sem=recv_sem.at[at],
            device_id=device,
            device_id_type=pl.DeviceIdType.MESH,
        )
        copy.start()
        started.append(copy)
        return copy

    loads[0].wait()
    for i in range(mask_ref.shape[0]):
        if i % (quarter // TILE) == 0:
            loads[1 + i // (quarter // TILE)].wait()
        for j in range(mask_ref.shape[1]):
            keep = jnp.full((TILE, TILE), mask_ref[i, j].astype(F32), F32).astype(BF16)
            rows, cols = pl.ds(i * TILE, TILE), pl.ds(j * TILE, TILE)
            masked[rows, cols] = factor_ref[rows, cols] * keep

    def rows_of(chip, core_there):
        start = pl.multiple_of((chip * CORES + core_there) * brows, brows)
        return masked[pl.ds(start, brows), :]

    first = 2 * (1 - bit0)
    second = 2 * bit0
    order = (first, first + 1, second, second + 1)
    a_copies, b_copies, near_copies = [], [], []
    near_chip = y

    def columns_of(q):
        return masked[pl.ds(pl.multiple_of(q * quarter, quarter), quarter), :]

    def forward(k):
        copies = []
        for d, other in enumerate(others):
            a_copies[k][d].wait_recv()
            b_send[k, d] = own[k, other] + a_recv[k, other]
            copies.append(send(b_send.at[k, d], b_recv.at[k, d], {"panel": other * CORES + core}))
        b_copies.append(copies)

    for k, q in enumerate(order):
        copies = []
        for other in others:
            a_send[k, other] = nt(rows_of(other, 1 - core), columns_of(q))
            if not started:
                pl.semaphore_wait(barrier, len(greeted))
            copies.append(send(a_send.at[k, other], a_recv.at[k, other], {"panel": partner}))
        a_copies.append(copies)
        for other in others:
            own[k, other] = nt(rows_of(other, core), columns_of(q))
        if k:
            forward(k - 1)
    forward(len(order) - 1)
    for k, q in enumerate(order):
        a_send[k, near_chip] = nt(rows_of(near_chip, 1 - core), columns_of(q))
        near_copies.append(
            send(a_send.at[k, near_chip], a_recv.at[k, near_chip], {"panel": partner})
        )
        own[k, near_chip] = nt(rows_of(near_chip, core), columns_of(q))
    for load in loads[1 + QUARTERS :]:
        load.wait()

    def map_of(level, child, start, size):
        rows = maps_ref[level, :, pl.ds(start, size)]
        at = lax.broadcasted_iota(jnp.int32, rows.shape, 0)
        return jnp.sum(jnp.where(at == child, rows, 0), axis=0, keepdims=True)

    def row_spread(level, child):
        window = max(brows, 128)
        start = pl.multiple_of(p * brows // window * window, 128)
        row = map_of(level, child, start, window)
        picked = row[:, :brows]
        for t in range(1, window // brows):
            here = (p % (window // brows)) == t
            picked = jnp.where(here, row[:, t * brows : (t + 1) * brows], picked)
        r = picked - p * fronts
        target = jnp.where(r >= srows, r - srows, brows + r)
        at = lax.broadcasted_iota(jnp.int32, (fronts, brows), 0)
        return jnp.where(at == target, 1.0, 0.0).astype(BF16)

    def column_spread(level, child, q):
        start = pl.multiple_of(q * quarter, quarter)
        row = map_of(level, child, start, quarter)
        block = lax.broadcasted_iota(jnp.int32, (1, quarter), 1) // brows
        r = row - (q * (quarter // brows) + block) * fronts
        target = jnp.where(r >= srows, block * brows + r - srows, quarter + block * srows + r)
        at = lax.broadcasted_iota(jnp.int32, (quarter + qsep, quarter), 0)
        return jnp.where(at == target, 1.0, 0.0).astype(BF16)

    def place(block, rows, columns):
        high, low = split(block)
        lifted = nn(rows, high) + nn(rows, low)
        high, low = split(lifted)
        border, sep = columns[:quarter], columns[quarter:]
        spread = nt(high, border) + nt(low, border)
        coupling = nt(sep, high[:brows]) + nt(sep, low[:brows])
        return spread, coupling

    def share_rows(w, *at):
        mine = w.at[(p, *at)]
        near = send(mine, mine, {"panel": partner})
        far = [
            (other * CORES + core, send(mine, mine, {"panel": other * CORES + core}))
            for other in others
        ]
        return near, far

    def relay_rows(w, near, far, *at):
        relays = []
        for d, (_, copy) in enumerate(far, 1):
            copy.wait_recv()
            slot = w.at[((y + chips - d) % chips * CORES + core, *at)]
            relays.append(send(slot, slot, {"panel": partner}))
        near.wait_recv()
        for relay in relays:
            relay.wait_recv()

    def coupled_rows(level, v):
        front = s // 2 ** (level + 1)
        gains = scale_ref[level, pl.ds(front, 1), :]
        rows = jnp.transpose(v[...].reshape(SEP, brows))
        return product(rows * gains, inverse_ref[level] * gains)

    child = s
    sibling = sub1
    rows_own, rows_far = row_spread(0, child), row_spread(0, sibling)

    def total(k):
        near_copies[k].wait_recv()
        for copy in b_copies[k]:
            copy.wait_recv()
        value = own[k, y] + a_recv[k, y]
        for d in range(chips - 1):
            value = value + b_recv[k, d]
        return value

    c_copies = []
    for k in range(2):
        c_send[k] = total(k)
        c_copies.append(send(c_send.at[k], c_recv.at[k], {"sub": sub1}))
    v_shares, w_shares = [], []
    for j in range(2):
        q = second + j
        spread_own, coupling_own = place(total(2 + j), rows_own, column_spread(0, child, q))
        c_copies[j].wait_recv()
        spread_far, coupling_far = place(c_recv[j], rows_far, column_spread(0, sibling, q))
        spread = spread_own + spread_far
        bb0[j] = spread[:brows]
        w0[p, j] = spread[brows:]
        v0[q] = coupling_own + coupling_far
        v_shares.append(send(v0.at[q], v0.at[q], {"sub": sub1}))
        w_shares.append(share_rows(w0, j))
    q = 2 * bit0 + bit1
    group = s // 8 * 8
    child1 = s // 2
    sibling1 = s // 4 * 2 + (1 - bit1)
    child2 = s // 4
    sibling2 = s // 8 * 2 + (1 - bit2)
    relay_rows(w0, *w_shares[0], 0)
    for v_share in v_shares:
        v_share.wait_recv()
    coupled = coupled_rows(0, v0)
    relay_rows(w0, *w_shares[1], 1)

    def updated(j):
        return bb0[j] - product(coupled, w0[:, j].reshape(SEP, quarter))

    d_send[...] = updated(1 - bit1)
    copy = send(d_send, d_recv, {"sub": sub2})
    schur = updated(bit1)
    for level, child, sibling, received, w, v in (
        (1, child1, sibling1, d_recv, w1, v1),
        (2, child2, sibling2, e_recv, w2, v2),
    ):
        spread_own, coupling_own = place(
            schur, row_spread(level, child), column_spread(level, child, q)
        )
        rows_far, columns_far = row_spread(level, sibling), column_spread(level, sibling, q)
        copy.wait_recv()
        spread_far, coupling_far = place(received[...], rows_far, columns_far)
        spread = spread_own + spread_far
        w[p] = spread[brows:]
        v[q] = coupling_own + coupling_far
        mine = v.at[q]
        v_copies = [send(mine, mine, {"sub": sub}) for sub in (sub3, sub1, sub2)]
        near, far = share_rows(w)
        for v_copy in v_copies:
            v_copy.wait_recv()
        coupled = coupled_rows(level, v)
        relay_rows(w, near, far)
        schur = spread[:brows] - product(coupled, w[...].reshape(SEP, quarter))
        if level == 1:
            e_send[...] = schur
            copy = send(e_send, e_recv, {"sub": sub4})
    fin[q] = schur
    half = brows // 2
    quarter1, quarter2 = 2 * (1 - bit0) + bit1, 2 * bit0 + 1 - bit1
    stores = []

    def part(at, h):
        return fin.at[at, pl.ds(h * half, half)]

    def store(at):
        columns = pl.ds(pl.multiple_of(at * quarter, quarter), quarter)
        copy = pltpu.make_async_copy(
            fin.at[at], out_ref.at[0, :, columns], store_sem.at[len(stores)]
        )
        copy.start()
        stores.append(copy)

    near = [send(part(q, h), part(q, h), {"sub": sub1}) for h in (0, 1)]
    far = [send(part(q, h), part(q, h), {"sub": sub2}) for h in (1, 0)]
    store(q)
    near[0].wait_recv()
    upper = send(part(quarter1, 0), part(quarter1, 0), {"sub": sub2})
    far[0].wait_recv()
    lower = send(part(quarter2, 1), part(quarter2, 1), {"sub": sub1})
    near[1].wait_recv()
    store(quarter1)
    far[1].wait_recv()
    store(quarter2)
    upper.wait_recv()
    lower.wait_recv()
    store(2 * (1 - bit0) + 1 - bit1)
    for copy in stores:
        copy.wait()
    for copy in started:
        copy.wait_send()


def body(border_factor, tile_mask, front_maps, sep_inverse, sep_scale):
    panels = lax.axis_size("panel")
    chips = panels // CORES
    brows = BORDER // panels
    srows = SEP // panels
    quarter = BORDER // QUARTERS
    qsep = SEP // QUARTERS
    copies = 4 + 8 * (chips - 1) + 2 + 4 * (1 + 2 * (chips - 1)) + 2 + 6 + 2 + 6
    hbm = pl.BlockSpec(memory_space=pltpu.HBM)
    block = pltpu.VMEM((brows, quarter), F32)
    return pl.pallas_call(
        functools.partial(kernel, panels),
        out_shape=jax.ShapeDtypeStruct((1, brows, BORDER), F32),
        in_specs=[hbm] * 5,
        out_specs=hbm,
        scratch_shapes=[
            pltpu.SMEM(tile_mask.shape[1:], jnp.int32),
            pltpu.VMEM(border_factor.shape[1:], BF16),
            pltpu.VMEM(front_maps.shape, jnp.int32),
            pltpu.VMEM(sep_inverse.shape, F32),
            pltpu.VMEM(sep_scale.shape, F32),
            pltpu.SemaphoreType.DMA((1 + QUARTERS + 3,)),
            pltpu.SemaphoreType.DMA((QUARTERS,)),
            pltpu.VMEM((BORDER, border_factor.shape[2]), BF16),
            pltpu.VMEM((4, chips, brows, quarter), F32),
            pltpu.VMEM((4, chips, brows, quarter), F32),
            pltpu.VMEM((4, chips, brows, quarter), F32),
            pltpu.VMEM((4, chips - 1, brows, quarter), F32),
            pltpu.VMEM((4, chips - 1, brows, quarter), F32),
            pltpu.VMEM((2, brows, quarter), F32),
            pltpu.VMEM((2, brows, quarter), F32),
            pltpu.VMEM((panels, 2, srows, quarter), F32),
            pltpu.VMEM((panels, srows, quarter), F32),
            pltpu.VMEM((panels, srows, quarter), F32),
            pltpu.VMEM((QUARTERS, qsep, brows), F32),
            pltpu.VMEM((QUARTERS, qsep, brows), F32),
            pltpu.VMEM((QUARTERS, qsep, brows), F32),
            pltpu.VMEM((2, brows, quarter), F32),
            block,
            block,
            block,
            block,
            pltpu.VMEM((QUARTERS, brows, quarter), F32),
            pltpu.SemaphoreType.DMA((copies,)),
            pltpu.SemaphoreType.DMA((copies,)),
        ],
        compiler_params=pltpu.CompilerParams(
            collective_id=0, has_side_effects=True, vmem_limit_bytes=67043328
        ),
    )(tile_mask, border_factor, front_maps, sep_inverse, sep_scale)


def solution(mesh):
    return jax.shard_map(
        body,
        mesh=mesh,
        in_specs=(P("sub", None, "panel"), P("sub", None, "panel"), P(), P(), P()),
        out_specs=P("sub", "panel", None),
        check_vma=False,
    )
```

```python
import functools

import jax
import jax.numpy as jnp
from jax import lax
from jax.experimental import pallas as pl
from jax.experimental.pallas import tpu as pltpu
from jax.sharding import PartitionSpec as P

BORDER = 1024
SEP = 256
TILE = 128
LEVELS = 3
CORES = 2
QUARTERS = 4
F32 = jnp.float32
BF16 = jnp.bfloat16


def nn(a, b):
    return lax.dot_general(a, b, (((1,), (0,)), ((), ())), preferred_element_type=F32)


def nt(a, b):
    return lax.dot_general(a, b, (((1,), (1,)), ((), ())), preferred_element_type=F32)


def split(x):
    high = x.astype(BF16)
    return high, (x - high.astype(F32)).astype(BF16)


def product(a, b):
    a_high, a_low = split(a)
    b_high, b_low = split(b)
    return nn(a_high, b_high) + nn(a_high, b_low) + nn(a_low, b_high)


def kernel(
    panels,
    mask_hbm,
    factor_hbm,
    maps_hbm,
    inverse_hbm,
    scale_hbm,
    out_ref,
    mask_ref,
    factor_ref,
    maps_ref,
    inverse_ref,
    scale_ref,
    load_sem,
    store_sem,
    masked,
    a_send,
    a_recv,
    own,
    b_send,
    b_recv,
    c_send,
    c_recv,
    w0,
    w1,
    w2,
    v0,
    v1,
    v2,
    bb0,
    d_send,
    d_recv,
    e_send,
    e_recv,
    fin,
    send_sem,
    recv_sem,
):
    chips = panels // CORES
    brows = BORDER // panels
    srows = SEP // panels
    fronts = brows + srows
    quarter = BORDER // QUARTERS
    qsep = SEP // QUARTERS
    p = lax.axis_index("panel")
    s = lax.axis_index("sub")
    y, core = p // CORES, p % CORES
    bit0, bit1, bit2 = s % 2, s // 2 % 2, s // 4 % 2
    base = s - s % 8
    sub1 = base + bit2 * 4 + bit1 * 2 + (1 - bit0)
    sub2 = base + bit2 * 4 + (1 - bit1) * 2 + bit0
    sub3 = base + bit2 * 4 + (1 - bit1) * 2 + (1 - bit0)
    sub4 = base + (1 - bit2) * 4 + bit1 * 2 + bit0
    partner = y * CORES + 1 - core
    others = [(y + d) % chips for d in range(1, chips)]

    loads = [pltpu.make_async_copy(mask_hbm.at[0], mask_ref, load_sem.at[0])]
    for i in range(QUARTERS):
        rows = pl.ds(i * quarter, quarter)
        loads.append(
            pltpu.make_async_copy(factor_hbm.at[0, rows], factor_ref.at[rows], load_sem.at[1 + i])
        )
    for i, (src, dst) in enumerate(
        ((maps_hbm, maps_ref), (inverse_hbm, inverse_ref), (scale_hbm, scale_ref))
    ):
        loads.append(pltpu.make_async_copy(src, dst, load_sem.at[1 + QUARTERS + i]))
    for load in loads:
        load.start()

    barrier = pltpu.get_barrier_semaphore()
    greeted = [{"panel": partner}] + [
        {"panel": other * CORES + core} for other in others
    ] + [{"sub": sub} for sub in (sub1, sub2, sub3, sub4)]
    for device in greeted:
        pl.semaphore_signal(barrier, inc=1, device_id=device, device_id_type=pl.DeviceIdType.MESH)

    started = []

    def send(src, dst, device):
        at = len(started)
        copy = pltpu.make_async_remote_copy(
            src_ref=src,
            dst_ref=dst,
            send_sem=send_sem.at[at],
            recv_sem=recv_sem.at[at],
            device_id=device,
            device_id_type=pl.DeviceIdType.MESH,
        )
        copy.start()
        started.append(copy)
        return copy

    loads[0].wait()
    for i in range(mask_ref.shape[0]):
        if i % (quarter // TILE) == 0:
            loads[1 + i // (quarter // TILE)].wait()
        for j in range(mask_ref.shape[1]):
            keep = jnp.full((TILE, TILE), mask_ref[i, j].astype(F32), F32).astype(BF16)
            rows, cols = pl.ds(i * TILE, TILE), pl.ds(j * TILE, TILE)
            masked[rows, cols] = factor_ref[rows, cols] * keep

    def rows_of(chip, core_there):
        start = pl.multiple_of((chip * CORES + core_there) * brows, brows)
        return masked[pl.ds(start, brows), :]

    first = 2 * (1 - bit0)
    second = 2 * bit0
    order = (first, first + 1, second, second + 1)
    a_copies, b_copies, near_copies = [], [], []
    near_chip = y

    def columns_of(q):
        return masked[pl.ds(pl.multiple_of(q * quarter, quarter), quarter), :]

    def forward(k):
        copies = []
        for d, other in enumerate(others):
            a_copies[k][d].wait_recv()
            b_send[k, d] = own[k, other] + a_recv[k, other]
            copies.append(send(b_send.at[k, d], b_recv.at[k, d], {"panel": other * CORES + core}))
        b_copies.append(copies)

    for k, q in enumerate(order):
        copies = []
        for other in others:
            a_send[k, other] = nt(rows_of(other, 1 - core), columns_of(q))
            if not started:
                pl.semaphore_wait(barrier, len(greeted))
            copies.append(send(a_send.at[k, other], a_recv.at[k, other], {"panel": partner}))
        a_copies.append(copies)
        for other in others:
            own[k, other] = nt(rows_of(other, core), columns_of(q))
        if k:
            forward(k - 1)
    forward(len(order) - 1)
    for k, q in enumerate(order):
        a_send[k, near_chip] = nt(rows_of(near_chip, 1 - core), columns_of(q))
        near_copies.append(
            send(a_send.at[k, near_chip], a_recv.at[k, near_chip], {"panel": partner})
        )
        own[k, near_chip] = nt(rows_of(near_chip, core), columns_of(q))
    for load in loads[1 + QUARTERS :]:
        load.wait()

    def map_of(level, child, start, size):
        rows = maps_ref[level, :, pl.ds(start, size)]
        at = lax.broadcasted_iota(jnp.int32, rows.shape, 0)
        return jnp.sum(jnp.where(at == child, rows, 0), axis=0, keepdims=True)

    def row_spread(level, child):
        window = max(brows, 128)
        start = pl.multiple_of(p * brows // window * window, 128)
        row = map_of(level, child, start, window)
        picked = row[:, :brows]
        for t in range(1, window // brows):
            here = (p % (window // brows)) == t
            picked = jnp.where(here, row[:, t * brows : (t + 1) * brows], picked)
        r = picked - p * fronts
        target = jnp.where(r >= srows, r - srows, brows + r)
        at = lax.broadcasted_iota(jnp.int32, (fronts, brows), 0)
        return jnp.where(at == target, 1.0, 0.0).astype(BF16)

    def column_spread(level, child, q):
        start = pl.multiple_of(q * quarter, quarter)
        row = map_of(level, child, start, quarter)
        block = lax.broadcasted_iota(jnp.int32, (1, quarter), 1) // brows
        r = row - (q * (quarter // brows) + block) * fronts
        target = jnp.where(r >= srows, block * brows + r - srows, quarter + block * srows + r)
        at = lax.broadcasted_iota(jnp.int32, (quarter + qsep, quarter), 0)
        return jnp.where(at == target, 1.0, 0.0).astype(BF16)

    half = brows // 2

    def lift(block, rows):
        high, low = split(block)
        return nn(rows, high) + nn(rows, low)

    def place(block, rows, columns):
        return settle(lift(block, rows), columns)

    def settle(lifted, columns):
        high, low = split(lifted)
        border, sep = columns[:quarter], columns[quarter:]
        spread = nt(high, border) + nt(low, border)
        coupling = nt(sep, high[:brows]) + nt(sep, low[:brows])
        return spread, coupling

    def share_rows(w, *at):
        mine = w.at[(p, *at)]
        near = send(mine, mine, {"panel": partner})
        far = [
            (other * CORES + core, send(mine, mine, {"panel": other * CORES + core}))
            for other in others
        ]
        return near, far

    def relay_rows(w, near, far, *at):
        relays = []
        for d, (_, copy) in enumerate(far, 1):
            copy.wait_recv()
            slot = w.at[((y + chips - d) % chips * CORES + core, *at)]
            relays.append(send(slot, slot, {"panel": partner}))
        near.wait_recv()
        for relay in relays:
            relay.wait_recv()

    def coupled_rows(level, v):
        front = s // 2 ** (level + 1)
        gains = scale_ref[level, pl.ds(front, 1), :]
        rows = jnp.transpose(v[...].reshape(SEP, brows))
        return product(rows * gains, inverse_ref[level] * gains)

    child = s
    sibling = sub1
    rows_own, rows_far = row_spread(0, child), row_spread(0, sibling)

    def total(k):
        near_copies[k].wait_recv()
        for copy in b_copies[k]:
            copy.wait_recv()
        value = own[k, y] + a_recv[k, y]
        for d in range(chips - 1):
            value = value + b_recv[k, d]
        return value

    c_copies = []
    for k in range(2):
        c_send[k] = total(k)
        c_copies.append(send(c_send.at[k], c_recv.at[k], {"sub": sub1}))
    v_shares, w_shares = [], []
    for j in range(2):
        q = second + j
        spread_own, coupling_own = place(total(2 + j), rows_own, column_spread(0, child, q))
        c_copies[j].wait_recv()
        spread_far, coupling_far = place(c_recv[j], rows_far, column_spread(0, sibling, q))
        spread = spread_own + spread_far
        bb0[j] = spread[:brows]
        w0[p, j] = spread[brows:]
        v0[q] = coupling_own + coupling_far
        v_shares.append(send(v0.at[q], v0.at[q], {"sub": sub1}))
        w_shares.append(share_rows(w0, j))
    q = 2 * bit0 + bit1
    group = s // 8 * 8
    child1 = s // 2
    sibling1 = s // 4 * 2 + (1 - bit1)
    child2 = s // 4
    sibling2 = s // 8 * 2 + (1 - bit2)
    relay_rows(w0, *w_shares[0], 0)
    for v_share in v_shares:
        v_share.wait_recv()
    coupled = coupled_rows(0, v0)
    relay_rows(w0, *w_shares[1], 1)

    def updated(j):
        return bb0[j] - product(coupled, w0[:, j].reshape(SEP, quarter))

    def send_halves(src, dst, sub):
        return [
            send(src.at[pl.ds(h * half, half)], dst.at[pl.ds(h * half, half)], {"sub": sub})
            for h in range(2)
        ]

    d_send[...] = updated(1 - bit1)
    copies = send_halves(d_send, d_recv, sub2)
    schur = updated(bit1)
    for level, child, sibling, received, w, v in (
        (1, child1, sibling1, d_recv, w1, v1),
        (2, child2, sibling2, e_recv, w2, v2),
    ):
        spread_own, coupling_own = place(
            schur, row_spread(level, child), column_spread(level, child, q)
        )
        rows_far, columns_far = row_spread(level, sibling), column_spread(level, sibling, q)
        lifted = jnp.zeros((fronts, quarter), F32)
        for h, copy in enumerate(copies):
            copy.wait_recv()
            at = slice(h * half, (h + 1) * half)
            lifted = lifted + lift(received[at], rows_far[:, at])
        spread_far, coupling_far = settle(lifted, columns_far)
        spread = spread_own + spread_far
        w[p] = spread[brows:]
        v[q] = coupling_own + coupling_far
        mine = v.at[q]
        v_copies = [send(mine, mine, {"sub": sub}) for sub in (sub3, sub1, sub2)]
        near, far = share_rows(w)
        for v_copy in v_copies:
            v_copy.wait_recv()
        coupled = coupled_rows(level, v)
        relay_rows(w, near, far)
        schur = spread[:brows] - product(coupled, w[...].reshape(SEP, quarter))
        if level == 1:
            e_send[...] = schur
            copies = send_halves(e_send, e_recv, sub4)
    fin[q] = schur
    quarter1, quarter2 = 2 * (1 - bit0) + bit1, 2 * bit0 + 1 - bit1
    stores = []

    def part(at, h):
        return fin.at[at, pl.ds(h * half, half)]

    def store(at):
        columns = pl.ds(pl.multiple_of(at * quarter, quarter), quarter)
        copy = pltpu.make_async_copy(
            fin.at[at], out_ref.at[0, :, columns], store_sem.at[len(stores)]
        )
        copy.start()
        stores.append(copy)

    near = [send(part(q, h), part(q, h), {"sub": sub1}) for h in (0, 1)]
    far = [send(part(q, h), part(q, h), {"sub": sub2}) for h in (1, 0)]
    store(q)
    near[0].wait_recv()
    upper = send(part(quarter1, 0), part(quarter1, 0), {"sub": sub2})
    far[0].wait_recv()
    lower = send(part(quarter2, 1), part(quarter2, 1), {"sub": sub1})
    near[1].wait_recv()
    store(quarter1)
    far[1].wait_recv()
    store(quarter2)
    upper.wait_recv()
    lower.wait_recv()
    store(2 * (1 - bit0) + 1 - bit1)
    for copy in stores:
        copy.wait()
    for copy in started:
        copy.wait_send()


def body(border_factor, tile_mask, front_maps, sep_inverse, sep_scale):
    panels = lax.axis_size("panel")
    chips = panels // CORES
    brows = BORDER // panels
    srows = SEP // panels
    quarter = BORDER // QUARTERS
    qsep = SEP // QUARTERS
    copies = 4 + 8 * (chips - 1) + 2 + 4 * (1 + 2 * (chips - 1)) + 2 + 6 + 4 + 6
    hbm = pl.BlockSpec(memory_space=pltpu.HBM)
    block = pltpu.VMEM((brows, quarter), F32)
    return pl.pallas_call(
        functools.partial(kernel, panels),
        out_shape=jax.ShapeDtypeStruct((1, brows, BORDER), F32),
        in_specs=[hbm] * 5,
        out_specs=hbm,
        scratch_shapes=[
            pltpu.SMEM(tile_mask.shape[1:], jnp.int32),
            pltpu.VMEM(border_factor.shape[1:], BF16),
            pltpu.VMEM(front_maps.shape, jnp.int32),
            pltpu.VMEM(sep_inverse.shape, F32),
            pltpu.VMEM(sep_scale.shape, F32),
            pltpu.SemaphoreType.DMA((1 + QUARTERS + 3,)),
            pltpu.SemaphoreType.DMA((QUARTERS,)),
            pltpu.VMEM((BORDER, border_factor.shape[2]), BF16),
            pltpu.VMEM((4, chips, brows, quarter), F32),
            pltpu.VMEM((4, chips, brows, quarter), F32),
            pltpu.VMEM((4, chips, brows, quarter), F32),
            pltpu.VMEM((4, chips - 1, brows, quarter), F32),
            pltpu.VMEM((4, chips - 1, brows, quarter), F32),
            pltpu.VMEM((2, brows, quarter), F32),
            pltpu.VMEM((2, brows, quarter), F32),
            pltpu.VMEM((panels, 2, srows, quarter), F32),
            pltpu.VMEM((panels, srows, quarter), F32),
            pltpu.VMEM((panels, srows, quarter), F32),
            pltpu.VMEM((QUARTERS, qsep, brows), F32),
            pltpu.VMEM((QUARTERS, qsep, brows), F32),
            pltpu.VMEM((QUARTERS, qsep, brows), F32),
            pltpu.VMEM((2, brows, quarter), F32),
            block,
            block,
            block,
            block,
            pltpu.VMEM((QUARTERS, brows, quarter), F32),
            pltpu.SemaphoreType.DMA((copies,)),
            pltpu.SemaphoreType.DMA((copies,)),
        ],
        compiler_params=pltpu.CompilerParams(
            collective_id=0, has_side_effects=True, vmem_limit_bytes=67043328
        ),
    )(tile_mask, border_factor, front_maps, sep_inverse, sep_scale)


def solution(mesh):
    return jax.shard_map(
        body,
        mesh=mesh,
        in_specs=(P("sub", None, "panel"), P("sub", None, "panel"), P(), P(), P()),
        out_specs=P("sub", "panel", None),
        check_vma=False,
    )
```

```python
import functools

import jax
import jax.numpy as jnp
from jax import lax
from jax.experimental import pallas as pl
from jax.experimental.pallas import tpu as pltpu
from jax.sharding import PartitionSpec as P

BORDER = 1024
SEP = 256
TILE = 128
LEVELS = 3
CORES = 2
QUARTERS = 4
F32 = jnp.float32
BF16 = jnp.bfloat16


def nn(a, b):
    return lax.dot_general(a, b, (((1,), (0,)), ((), ())), preferred_element_type=F32)


def nt(a, b):
    return lax.dot_general(a, b, (((1,), (1,)), ((), ())), preferred_element_type=F32)


def split(x):
    high = x.astype(BF16)
    return high, (x - high.astype(F32)).astype(BF16)


def product(a, b):
    a_high, a_low = split(a)
    b_high, b_low = split(b)
    return nn(a_high, b_high) + nn(a_high, b_low) + nn(a_low, b_high)


def kernel(
    panels,
    mask_hbm,
    factor_hbm,
    maps_hbm,
    inverse_hbm,
    scale_hbm,
    out_ref,
    mask_ref,
    factor_ref,
    maps_ref,
    inverse_ref,
    scale_ref,
    load_sem,
    store_sem,
    masked,
    a_send,
    a_recv,
    own,
    b_send,
    b_recv,
    c_send,
    c_recv,
    w0,
    w1,
    w2,
    v0,
    v1,
    v2,
    bb0,
    d_send,
    d_recv,
    e_send,
    e_recv,
    fin,
    send_sem,
    recv_sem,
):
    chips = panels // CORES
    brows = BORDER // panels
    srows = SEP // panels
    fronts = brows + srows
    quarter = BORDER // QUARTERS
    qsep = SEP // QUARTERS
    p = lax.axis_index("panel")
    s = lax.axis_index("sub")
    y, core = p // CORES, p % CORES
    bit0, bit1, bit2 = s % 2, s // 2 % 2, s // 4 % 2
    base = s - s % 8
    sub1 = base + bit2 * 4 + bit1 * 2 + (1 - bit0)
    sub2 = base + bit2 * 4 + (1 - bit1) * 2 + bit0
    sub3 = base + bit2 * 4 + (1 - bit1) * 2 + (1 - bit0)
    sub4 = base + (1 - bit2) * 4 + bit1 * 2 + bit0
    partner = y * CORES + 1 - core
    others = [(y + d) % chips for d in range(1, chips)]

    loads = [pltpu.make_async_copy(mask_hbm.at[0], mask_ref, load_sem.at[0])]
    for i in range(QUARTERS):
        rows = pl.ds(i * quarter, quarter)
        loads.append(
            pltpu.make_async_copy(factor_hbm.at[0, rows], factor_ref.at[rows], load_sem.at[1 + i])
        )
    for i, (src, dst) in enumerate(
        ((maps_hbm, maps_ref), (inverse_hbm, inverse_ref), (scale_hbm, scale_ref))
    ):
        loads.append(pltpu.make_async_copy(src, dst, load_sem.at[1 + QUARTERS + i]))
    for load in loads:
        load.start()

    barrier = pltpu.get_barrier_semaphore()
    greeted = [{"panel": partner}] + [
        {"panel": other * CORES + core} for other in others
    ] + [{"sub": sub} for sub in (sub1, sub2, sub3, sub4)]
    for device in greeted:
        pl.semaphore_signal(barrier, inc=1, device_id=device, device_id_type=pl.DeviceIdType.MESH)

    started = []

    def send(src, dst, device):
        at = len(started)
        copy = pltpu.make_async_remote_copy(
            src_ref=src,
            dst_ref=dst,
            send_sem=send_sem.at[at],
            recv_sem=recv_sem.at[at],
            device_id=device,
            device_id_type=pl.DeviceIdType.MESH,
        )
        copy.start()
        started.append(copy)
        return copy

    loads[0].wait()
    for i in range(mask_ref.shape[0]):
        if i % (quarter // TILE) == 0:
            loads[1 + i // (quarter // TILE)].wait()
        for j in range(mask_ref.shape[1]):
            keep = jnp.full((TILE, TILE), mask_ref[i, j].astype(F32), F32).astype(BF16)
            rows, cols = pl.ds(i * TILE, TILE), pl.ds(j * TILE, TILE)
            masked[rows, cols] = factor_ref[rows, cols] * keep

    def rows_of(chip, core_there):
        start = pl.multiple_of((chip * CORES + core_there) * brows, brows)
        return masked[pl.ds(start, brows), :]

    first = 2 * (1 - bit0)
    second = 2 * bit0
    order = (first, first + 1, second, second + 1)
    a_copies, b_copies, near_copies = [], [], []
    near_chip = y

    def columns_of(q):
        return masked[pl.ds(pl.multiple_of(q * quarter, quarter), quarter), :]

    def forward(k):
        copies = []
        for d, other in enumerate(others):
            a_copies[k][d].wait_recv()
            b_send[k, d] = own[k, other] + a_recv[k, other]
            copies.append(send(b_send.at[k, d], b_recv.at[k, d], {"panel": other * CORES + core}))
        b_copies.append(copies)

    for k, q in enumerate(order):
        copies = []
        for other in others:
            a_send[k, other] = nt(rows_of(other, 1 - core), columns_of(q))
            if not started:
                pl.semaphore_wait(barrier, len(greeted))
            copies.append(send(a_send.at[k, other], a_recv.at[k, other], {"panel": partner}))
        a_copies.append(copies)
        for other in others:
            own[k, other] = nt(rows_of(other, core), columns_of(q))
        if k:
            forward(k - 1)
    forward(len(order) - 1)
    for k, q in enumerate(order):
        a_send[k, near_chip] = nt(rows_of(near_chip, 1 - core), columns_of(q))
        near_copies.append(
            send(a_send.at[k, near_chip], a_recv.at[k, near_chip], {"panel": partner})
        )
        own[k, near_chip] = nt(rows_of(near_chip, core), columns_of(q))
    for load in loads[1 + QUARTERS :]:
        load.wait()

    def map_of(level, child, start, size):
        rows = maps_ref[level, :, pl.ds(start, size)]
        at = lax.broadcasted_iota(jnp.int32, rows.shape, 0)
        return jnp.sum(jnp.where(at == child, rows, 0), axis=0, keepdims=True)

    def row_spread(level, child):
        window = max(brows, 128)
        start = pl.multiple_of(p * brows // window * window, 128)
        row = map_of(level, child, start, window)
        picked = row[:, :brows]
        for t in range(1, window // brows):
            here = (p % (window // brows)) == t
            picked = jnp.where(here, row[:, t * brows : (t + 1) * brows], picked)
        r = picked - p * fronts
        target = jnp.where(r >= srows, r - srows, brows + r)
        at = lax.broadcasted_iota(jnp.int32, (fronts, brows), 0)
        return jnp.where(at == target, 1.0, 0.0).astype(BF16)

    def column_spread(level, child, q):
        start = pl.multiple_of(q * quarter, quarter)
        row = map_of(level, child, start, quarter)
        block = lax.broadcasted_iota(jnp.int32, (1, quarter), 1) // brows
        r = row - (q * (quarter // brows) + block) * fronts
        target = jnp.where(r >= srows, block * brows + r - srows, quarter + block * srows + r)
        at = lax.broadcasted_iota(jnp.int32, (quarter + qsep, quarter), 0)
        return jnp.where(at == target, 1.0, 0.0).astype(BF16)

    half = brows // 2

    def lift(block, rows):
        high, low = split(block)
        return nn(rows, high) + nn(rows, low)

    def place(block, rows, columns):
        return settle(lift(block, rows), columns)

    def settle(lifted, columns):
        high, low = split(lifted)
        border, sep = columns[:quarter], columns[quarter:]
        spread = nt(high, border) + nt(low, border)
        coupling = nt(sep, high[:brows]) + nt(sep, low[:brows])
        return spread, coupling

    def share_rows(w, *at):
        mine = w.at[(p, *at)]
        near = send(mine, mine, {"panel": partner})
        far = [
            (other * CORES + core, send(mine, mine, {"panel": other * CORES + core}))
            for other in others
        ]
        return near, far

    def relay_rows(w, near, far, *at):
        relays = []
        for d, (_, copy) in enumerate(far, 1):
            copy.wait_recv()
            slot = w.at[((y + chips - d) % chips * CORES + core, *at)]
            relays.append(send(slot, slot, {"panel": partner}))
        near.wait_recv()
        for relay in relays:
            relay.wait_recv()

    def coupled_rows(level, v):
        front = s // 2 ** (level + 1)
        gains = scale_ref[level, pl.ds(front, 1), :]
        rows = jnp.transpose(v[...].reshape(SEP, brows))
        return product(rows * gains, inverse_ref[level] * gains)

    child = s
    sibling = sub1
    rows_own, rows_far = row_spread(0, child), row_spread(0, sibling)

    def total(k):
        near_copies[k].wait_recv()
        for copy in b_copies[k]:
            copy.wait_recv()
        value = own[k, y] + a_recv[k, y]
        for d in range(chips - 1):
            value = value + b_recv[k, d]
        return value

    c_copies = []
    for k in range(2):
        c_send[k] = total(k)
        c_copies.append(send(c_send.at[k], c_recv.at[k], {"sub": sub1}))
    v_shares, w_shares = [], []
    for j in range(2):
        q = second + j
        spread_own, coupling_own = place(total(2 + j), rows_own, column_spread(0, child, q))
        c_copies[j].wait_recv()
        spread_far, coupling_far = place(c_recv[j], rows_far, column_spread(0, sibling, q))
        spread = spread_own + spread_far
        bb0[j] = spread[:brows]
        w0[p, j] = spread[brows:]
        v0[q] = coupling_own + coupling_far
        v_shares.append(send(v0.at[q], v0.at[q], {"sub": sub1}))
        w_shares.append(share_rows(w0, j))
    q = 2 * bit0 + bit1
    group = s // 8 * 8
    child1 = s // 2
    sibling1 = s // 4 * 2 + (1 - bit1)
    child2 = s // 4
    sibling2 = s // 8 * 2 + (1 - bit2)
    relay_rows(w0, *w_shares[0], 0)
    for v_share in v_shares:
        v_share.wait_recv()
    coupled = coupled_rows(0, v0)
    relay_rows(w0, *w_shares[1], 1)

    def updated(j):
        return bb0[j] - product(coupled, w0[:, j].reshape(SEP, quarter))

    def send_halves(src, dst, sub):
        return [
            send(src.at[pl.ds(h * half, half)], dst.at[pl.ds(h * half, half)], {"sub": sub})
            for h in range(2)
        ]

    d_send[...] = updated(1 - bit1)
    copies = send_halves(d_send, d_recv, sub2)
    schur = updated(bit1)
    for level, child, sibling, received, w, v in (
        (1, child1, sibling1, d_recv, w1, v1),
        (2, child2, sibling2, e_recv, w2, v2),
    ):
        spread_own, coupling_own = place(
            schur, row_spread(level, child), column_spread(level, child, q)
        )
        rows_far, columns_far = row_spread(level, sibling), column_spread(level, sibling, q)
        lifted = jnp.zeros((fronts, quarter), F32)
        for h, copy in enumerate(copies):
            copy.wait_recv()
            at = slice(h * half, (h + 1) * half)
            lifted = lifted + lift(received[at], rows_far[:, at])
        spread_far, coupling_far = settle(lifted, columns_far)
        spread = spread_own + spread_far
        w[p] = spread[brows:]
        v[q] = coupling_own + coupling_far
        mine = v.at[q]
        v_copies = [send(mine, mine, {"sub": sub}) for sub in (sub3, sub1, sub2)]
        near, far = share_rows(w)
        for v_copy in v_copies:
            v_copy.wait_recv()
        coupled = coupled_rows(level, v)
        relay_rows(w, near, far)
        schur = spread[:brows] - product(coupled, w[...].reshape(SEP, quarter))
        if level == 1:
            e_send[...] = schur
            copies = send_halves(e_send, e_recv, sub4)
    fin[q] = schur
    quarter1, quarter2 = 2 * (1 - bit0) + bit1, 2 * bit0 + 1 - bit1
    stores = []

    def part(at, h):
        return fin.at[at, pl.ds(h * half, half)]

    def store(at):
        copy = pltpu.make_async_copy(fin.at[at], out_ref.at[at], store_sem.at[len(stores)])
        copy.start()
        stores.append(copy)

    near = [send(part(q, h), part(q, h), {"sub": sub1}) for h in (0, 1)]
    far = [send(part(q, h), part(q, h), {"sub": sub2}) for h in (1, 0)]
    store(q)
    near[0].wait_recv()
    upper = send(part(quarter1, 0), part(quarter1, 0), {"sub": sub2})
    far[0].wait_recv()
    lower = send(part(quarter2, 1), part(quarter2, 1), {"sub": sub1})
    near[1].wait_recv()
    store(quarter1)
    far[1].wait_recv()
    store(quarter2)
    upper.wait_recv()
    lower.wait_recv()
    store(2 * (1 - bit0) + 1 - bit1)
    for copy in stores:
        copy.wait()
    for copy in started:
        copy.wait_send()


def body(border_factor, tile_mask, front_maps, sep_inverse, sep_scale):
    panels = lax.axis_size("panel")
    chips = panels // CORES
    brows = BORDER // panels
    srows = SEP // panels
    quarter = BORDER // QUARTERS
    qsep = SEP // QUARTERS
    copies = 4 + 8 * (chips - 1) + 2 + 4 * (1 + 2 * (chips - 1)) + 2 + 6 + 4 + 6
    hbm = pl.BlockSpec(memory_space=pltpu.HBM)
    block = pltpu.VMEM((brows, quarter), F32)
    quarters = pl.pallas_call(
        functools.partial(kernel, panels),
        out_shape=jax.ShapeDtypeStruct((QUARTERS, brows, quarter), F32),
        in_specs=[hbm] * 5,
        out_specs=hbm,
        scratch_shapes=[
            pltpu.SMEM(tile_mask.shape[1:], jnp.int32),
            pltpu.VMEM(border_factor.shape[1:], BF16),
            pltpu.VMEM(front_maps.shape, jnp.int32),
            pltpu.VMEM(sep_inverse.shape, F32),
            pltpu.VMEM(sep_scale.shape, F32),
            pltpu.SemaphoreType.DMA((1 + QUARTERS + 3,)),
            pltpu.SemaphoreType.DMA((QUARTERS,)),
            pltpu.VMEM((BORDER, border_factor.shape[2]), BF16),
            pltpu.VMEM((4, chips, brows, quarter), F32),
            pltpu.VMEM((4, chips, brows, quarter), F32),
            pltpu.VMEM((4, chips, brows, quarter), F32),
            pltpu.VMEM((4, chips - 1, brows, quarter), F32),
            pltpu.VMEM((4, chips - 1, brows, quarter), F32),
            pltpu.VMEM((2, brows, quarter), F32),
            pltpu.VMEM((2, brows, quarter), F32),
            pltpu.VMEM((panels, 2, srows, quarter), F32),
            pltpu.VMEM((panels, srows, quarter), F32),
            pltpu.VMEM((panels, srows, quarter), F32),
            pltpu.VMEM((QUARTERS, qsep, brows), F32),
            pltpu.VMEM((QUARTERS, qsep, brows), F32),
            pltpu.VMEM((QUARTERS, qsep, brows), F32),
            pltpu.VMEM((2, brows, quarter), F32),
            block,
            block,
            block,
            block,
            pltpu.VMEM((QUARTERS, brows, quarter), F32),
            pltpu.SemaphoreType.DMA((copies,)),
            pltpu.SemaphoreType.DMA((copies,)),
        ],
        compiler_params=pltpu.CompilerParams(
            collective_id=0, has_side_effects=True, vmem_limit_bytes=67043328
        ),
    )(tile_mask, border_factor, front_maps, sep_inverse, sep_scale)

    def join(quarters_ref, out_ref):
        for t in range(QUARTERS):
            out_ref[0, :, t * quarter : (t + 1) * quarter] = quarters_ref[t]

    steps = 2
    return pl.pallas_call(
        join,
        grid=(steps,),
        out_shape=jax.ShapeDtypeStruct((1, brows, BORDER), F32),
        in_specs=[pl.BlockSpec((QUARTERS, brows // steps, quarter), lambda i: (0, i, 0))],
        out_specs=pl.BlockSpec((1, brows // steps, BORDER), lambda i: (0, i, 0)),
    )(quarters)


def solution(mesh):
    return jax.shard_map(
        body,
        mesh=mesh,
        in_specs=(P("sub", None, "panel"), P("sub", None, "panel"), P(), P(), P()),
        out_specs=P("sub", "panel", None),
        check_vma=False,
    )
```
